32 devices in a mesh: groups: 2 (over y), tile: 4 (over z), vec: 4 (over x, core).
Axes of the slice: x: 2, y: 2, z: 4, core: 2. Of those that a mesh axis runs over, the one named last changes fastest.
Arguments:
- vectors: float32 [2, 256, 3, 8192], P(None, 'vec', None, ('groups', 'tile')), parts along dimension 3, may hold values from -6 to 6
- links: float32 [3, 2, 3, 3, 8192], P(None, None, None, None, ('groups', 'tile')), parts along dimension 4, may hold values from -2.5 to 2.5
- momenta: int32 [8, 3], replicated, may hold values from -2 to 2
- directions: int32 [2], replicated, may hold values from 0 to 5
Outputs:
- elementals: float32 [512, 2, 2, 8, 256], P(('groups', 'tile'), None, None, None, 'vec'), parts along dimension 0
The draws below stay inside these ranges and needn't reach their ends.
There are 2 independent parts, one for each index of `groups`. The reference program is written for one: setup_inputs(seed, part) draws one part's arguments, and reference() takes and returns one part's arrays. A program takes and returns all parts, laid end to end along the dimension named above; an argument that names none is the same for every part. Nothing has to cross between parts.
Inputs may be any that keep to these rules, and one draw needn't show every extreme that they name: directions 0, 1, 2 step forward along the first, second, third dimension; 3, 4, 5 step backward along them.
All inputs are finite; a program needn't handle non-finite values.
Results may differ from the reference program's by a relative error of at most 0.00012.
Values sent between devices are 32-bit elements; how exact they have to be, the bound alone decides.
A program may use at most 128 MiB of HBM per device.

```python
import math
import jax
import jax.numpy as jnp
from jax import lax

NV = 256
LY = 16
LZ = 32
ITERS = 4
NMOM = 8
NDISP = 2
LX = 8
NSITES = 4096


def set_ends(entries, stream_key, least, top_value):
    longest = entries.shape.index(max(entries.shape))
    spots = []
    for shift in (0, 1):
        where = [jax.random.randint(jax.random.fold_in(stream_key, axis), (), 0, length) for axis, length in enumerate(entries.shape)]
        where[longest] = (where[longest] + shift) % entries.shape[longest]
        spots.append(tuple(where))
    return entries.at[spots[0]].set(least).at[spots[1]].set(top_value)


def block_scale(key, shape, pieces, smallest, top_value):
    gain = 1.0
    for position, shards_of in pieces:
        steps = jax.random.uniform(jax.random.fold_in(jax.random.fold_in(key, 6), position), (shards_of,), jnp.float32, smallest / len(pieces), top_value / len(pieces))
        gain = gain * jnp.repeat(jnp.exp(steps), shape[position] // shards_of).reshape((-1,) + (1,) * (len(shape) - 1 - position))
    return gain


def noise(stream_key, shape, width, limit, split=(), kind=jnp.bfloat16):
    values = jax.random.normal(stream_key, shape, jnp.float32) * width
    if len(split) > 0:
        values = block_scale(stream_key, shape, split, -0.22, 0.18) * values
    return jnp.clip(values, min=-limit, max=limit).astype(kind)


def setup_inputs(seed: int = 0, part: int = 0) -> dict:
    seeds = jax.random.split(jax.random.key(seed), 5)
    part_keys = jax.random.split(jax.random.fold_in(seeds[4], part), 5)
    return {
        "vectors": noise(part_keys[0], (2, NV, 3, NSITES), 1.0, 6.0, ((1, 4), (3, 4)), jnp.float32),
        "links": noise(part_keys[1], (3, 2, 3, 3, NSITES), 6 ** -0.5, 2.5, ((4, 4),), jnp.float32),
        "momenta": set_ends(jax.random.randint(seeds[2], (NMOM, 3), -2, 3), jax.random.fold_in(seeds[2], 1), -2, 2).astype(jnp.int32),
        "directions": jax.random.randint(seeds[3], (NDISP,), 0, 6).astype(jnp.int32),
    }


hop_scale = 0.125

def link_apply(link_real, link_imag, field_real, field_imag, dagger):
    if dagger:
        link_real = jnp.swapaxes(link_real, 0, 1)
        link_imag = -jnp.swapaxes(link_imag, 0, 1)
    out_real = 0.0
    out_imag = 0.0
    for column in range(3):
        left_real = link_real[:, column][None]
        left_imag = link_imag[:, column][None]
        right_real = field_real[:, column][:, None]
        right_imag = field_imag[:, column][:, None]
        out_real = out_real + left_real * right_real - left_imag * right_imag
        out_imag = out_imag + left_real * right_imag + left_imag * right_real
    return (out_real, out_imag)

def hop_field(source, forward, backward):
    total_real = 0.0
    total_imag = 0.0
    for spatial in range(3):
        ahead = jnp.roll(source, -1, axis=3 + spatial)
        behind = jnp.roll(source, 1, axis=3 + spatial)
        ahead_real, ahead_imag = link_apply(forward[spatial][0], forward[spatial][1], ahead[0], ahead[1], False)
        behind_real, behind_imag = link_apply(backward[spatial][0], backward[spatial][1], behind[0], behind[1], True)
        total_real = total_real + ahead_real + behind_real
        total_imag = total_imag + ahead_imag + behind_imag
    return hop_scale * jnp.stack([total_real, total_imag])

def phases(momenta, flat_index, extent_x):
    plane_size = LY * LZ
    coord_x = flat_index // plane_size
    coord_y = flat_index % plane_size // LZ
    coord_z = flat_index % LZ
    part_x = jnp.mod(momenta[:, 0:1] * coord_x[None], extent_x).astype(jnp.float32) / extent_x
    part_y = jnp.mod(momenta[:, 1:2] * coord_y[None], LY).astype(jnp.float32) / LY
    part_z = jnp.mod(momenta[:, 2:3] * coord_z[None], LZ).astype(jnp.float32) / LZ
    angle = 2.0 * math.pi * (part_x + part_y + part_z)
    return (jnp.cos(angle), jnp.sin(angle))

def right_matrix(right_stack):
    disp_count = right_stack.shape[0]
    column_count = right_stack.shape[2]
    flat_real = right_stack[:, 0].reshape(disp_count, column_count, -1)
    flat_imag = right_stack[:, 1].reshape(disp_count, column_count, -1)
    real_side = jnp.concatenate([flat_real, flat_imag], axis=2)
    imag_side = jnp.concatenate([flat_imag, -flat_real], axis=2)
    return jnp.stack([real_side, imag_side], axis=1)

def twist_left(left_field, cos_row, sin_row):
    row_count = left_field.shape[1]
    twisted_real = cos_row * left_field[0] - sin_row * left_field[1]
    twisted_imag = cos_row * left_field[1] + sin_row * left_field[0]
    return jnp.concatenate([twisted_real.reshape(row_count, -1), twisted_imag.reshape(row_count, -1)], axis=1)

def elemental_each(left_field, right_mat, cosine, sine, norm_factor):

    def one_momentum(phase_pair):
        left_flat = twist_left(left_field, phase_pair[0], phase_pair[1])
        return jnp.einsum('ik,dcjk->idcj', left_flat, right_mat, precision=lax.Precision.HIGHEST)
    result = lax.map(one_momentum, (cosine, sine))
    return jnp.transpose(result, (1, 2, 3, 0, 4)) * norm_factor

def reference(vectors, links, momenta, directions):
    field = vectors.reshape(2, NV, 3, LX, LY, LZ)
    gauge = links.reshape(3, 2, 3, 3, LX, LY, LZ)
    forward = [gauge[spatial] for spatial in range(3)]
    backward = [jnp.roll(gauge[spatial], 1, axis=3 + spatial) for spatial in range(3)]
    previous = field
    current = hop_field(field, forward, backward)
    for order in range(ITERS - 1):
        following = 2.0 * hop_field(current, forward, backward) - previous
        previous, current = (current, following)
    filtered = current

    def make_branch(heading):
        spatial = heading % 3
        if heading < 3:

            def branch_fn():
                ahead = jnp.roll(filtered, -1, axis=3 + spatial)
                return jnp.stack(link_apply(forward[spatial][0], forward[spatial][1], ahead[0], ahead[1], False))
        else:

            def branch_fn():
                behind = jnp.roll(filtered, 1, axis=3 + spatial)
                return jnp.stack(link_apply(backward[spatial][0], backward[spatial][1], behind[0], behind[1], True))
        return branch_fn
    branches = [make_branch(heading) for heading in range(6)]
    displaced = [lax.switch(directions[disp_slot], branches) for disp_slot in range(NDISP)]
    right_stack = jnp.stack(displaced).reshape(NDISP, 2, NV, 3, NSITES)
    flat_index = jnp.arange(NSITES, dtype=jnp.int32)
    cosine, sine = phases(momenta, flat_index, LX)
    norm_factor = 1.0 / math.sqrt(3.0 * NSITES)
    right_mat = right_matrix(right_stack)
    return elemental_each(filtered.reshape(2, NV, 3, NSITES), right_mat, cosine, sine, norm_factor)
```

```python
import functools
import math

import jax
import jax.numpy as jnp
from jax import lax
from jax.experimental import pallas as pl
from jax.experimental.pallas import tpu as pltpu
from jax.sharding import PartitionSpec as P

LY = 16
LZ = 32
ITERS = 4
PLANE = LY * LZ
LANES = 128
PER_PLANE = PLANE // LANES
HOP_SCALE = 0.125
VMEM_LIMIT = 60 * 1024 * 1024
CORES = 2
MESH = pl.DeviceIdType.MESH


def lane_index(like):
    return lax.broadcasted_iota(jnp.int32, like.shape, len(like.shape) - 1)


def shift_z(value, step):
    axis = len(value.shape) - 1
    lane = lane_index(value) % LZ
    if step > 0:
        plain = pltpu.roll(value, LANES - 1, axis)
        wrapped = pltpu.roll(value, LZ - 1, axis)
        return jnp.where(lane == LZ - 1, wrapped, plain)
    plain = pltpu.roll(value, 1, axis)
    wrapped = pltpu.roll(value, LANES - LZ + 1, axis)
    return jnp.where(lane == 0, wrapped, plain)


def shift_y(value, other, step):
    axis = len(value.shape) - 1
    lane = lane_index(value)
    if step > 0:
        return pltpu.roll(jnp.where(lane < LZ, other, value), LANES - LZ, axis)
    return pltpu.roll(jnp.where(lane >= LANES - LZ, other, value), LZ, axis)


def in_plane(chunk, step):
    base = chunk // PER_PLANE * PER_PLANE
    return base + (chunk + step + PER_PLANE) % PER_PLANE


def link_row(links, chunk, spatial, part, row, column):
    index = (part * 3 + row) * 3 + column
    return links[chunk, spatial, index : index + 1, :]


def apply_link(links, chunk, spatial, dagger, field, total):
    for row in range(3):
        real, imag = total[row], total[3 + row]
        for column in range(3):
            a, b = (column, row) if dagger else (row, column)
            lr = link_row(links, chunk, spatial, 0, a, b)
            li = link_row(links, chunk, spatial, 1, a, b)
            vr, vi = field[column], field[3 + column]
            if dagger:
                dr = lr * vr + li * vi
                di = lr * vi - li * vr
            else:
                dr = lr * vr - li * vi
                di = lr * vi + li * vr
            real = dr if real is None else real + dr
            imag = di if imag is None else imag + di
        total[row], total[3 + row] = real, imag
    return total


def moved(read, chunk, spatial, step, ahead_x):
    if spatial == 0:
        return [read(ahead_x, comp) for comp in range(6)]
    if spatial == 1:
        other = in_plane(chunk, step)
        return [shift_y(read(chunk, comp), read(other, comp), step) for comp in range(6)]
    return [shift_z(read(chunk, comp), step) for comp in range(6)]


def remote(src, dst, send, recv, axis, device):
    return pltpu.make_async_remote_copy(
        src_ref=src,
        dst_ref=dst,
        send_sem=send,
        recv_sem=recv,
        device_id={axis: device},
        device_id_type=MESH,
    )


def greet(places):
    barrier = pltpu.get_barrier_semaphore()
    for axis, device in places:
        pl.semaphore_signal(barrier, inc=1, device_id={axis: device}, device_id_type=MESH)
    pl.semaphore_wait(barrier, len(places))


def spread_kernel(tiles, vecs, links_in, field_in, gathered, own_back, *scratch):
    field, first, second, pieces, links, back, *sems = scratch
    local_sem, link_z, link_x, link_p, link_f, out_sem, back_sem, x_sem, p_sem, f_sem = sems
    groups, every = field.shape[0], field.shape[1]
    chunks = every // tiles
    some = pieces.shape[2]
    me, vec = lax.axis_index("tile"), lax.axis_index("vec")
    partner = vec + 1 - 2 * (vec % CORES)
    others = vecs // CORES
    tile_at = lambda turn: (me + turn) % tiles
    vec_at = lambda turn: (vec + CORES * turn) % vecs
    slab = lambda tile: pl.ds(tile * chunks, chunks)

    greet(
        [("tile", tile_at(turn)) for turn in range(1, tiles)]
        + [("vec", vec_at(turn)) for turn in range(1, others)]
        + [("vec", partner)]
    )

    waits = []

    def begin(copy):
        copy.start()
        waits.append(copy)
        return copy

    own_links = pltpu.make_async_copy(links_in, pieces.at[me, vec], local_sem.at[0])
    own_links.start()
    links_z = [
        begin(remote(links_in, pieces.at[me, vec], link_z.at[0, turn], link_z.at[1, turn], "tile", tile_at(turn)))
        for turn in range(1, tiles)
    ]
    own_field, sent = [], []
    for group in range(groups):
        own_field.append(
            pltpu.make_async_copy(
                field_in.at[group, me], field.at[group, slab(me)], local_sem.at[1 + group]
            )
        )
        own_field[group].start()
        sent.append(
            [
                begin(
                    remote(
                        field_in.at[group, tile_at(turn)],
                        field.at[group, slab(me)],
                        out_sem.at[0, group, turn],
                        out_sem.at[1, group, turn],
                        "tile",
                        tile_at(turn),
                    )
                )
                for turn in range(1, tiles)
            ]
        )

    own_links.wait()
    for copy in links_z:
        copy.wait_recv()
    mine = pieces.at[:, vec]
    links_x = [
        begin(remote(mine, mine, link_x.at[0, turn], link_x.at[1, turn], "vec", vec_at(turn)))
        for turn in range(1, others)
    ]
    links_p = begin(remote(mine, mine, link_p.at[0], link_p.at[1], "vec", partner))
    links_f = []
    for turn in range(1, others):
        links_x[turn - 1].wait_recv()
        got = pieces.at[:, vec_at(others - turn)]
        links_f.append(
            begin(remote(got, got, link_f.at[0, turn], link_f.at[1, turn], "vec", partner))
        )
    links_p.wait_recv()
    for copy in links_f:
        copy.wait_recv()

    @pl.loop(0, every)
    def _(chunk):
        place = chunk % chunks
        links[chunk] = pieces[chunk // chunks, place // some, place % some]

    @pl.loop(0, every)
    def _(chunk):
        back[chunk, 0] = links[(chunk - PER_PLANE + every) % every, 0]
        back[chunk, 1] = shift_y(links[chunk, 1], links[in_plane(chunk, -1), 1], -1)
        back[chunk, 2] = shift_z(links[chunk, 2], -1)

    @pl.loop(0, chunks)
    def _(chunk):
        own_back[chunk] = back[me * chunks + chunk]

    def hop(source, previous, target):
        @pl.loop(0, every)
        def _(chunk):
            read = lambda at, comp: source[at, comp]
            total = [None] * 6
            for spatial in range(3):
                ahead = moved(read, chunk, spatial, 1, (chunk + PER_PLANE) % every)
                total = apply_link(links, chunk, spatial, False, ahead, total)
                behind = moved(
                    read, chunk, spatial, -1, (chunk - PER_PLANE + every) % every
                )
                total = apply_link(back, chunk, spatial, True, behind, total)
            for comp in range(6):
                if previous is None:
                    target[chunk, comp] = HOP_SCALE * total[comp]
                else:
                    target[chunk, comp] = (
                        2.0 * HOP_SCALE * total[comp] - previous[chunk, comp]
                    )

    returned, across = {}, {}

    def share(group, turn):
        if turn > 0:
            returned[group, turn].wait_recv()
        else:
            returned[group, turn].wait()
        at = gathered.at[vec, tile_at(tiles - turn), group]
        for step in range(1, others):
            across[group, turn, step] = begin(
                remote(
                    at, at, x_sem.at[0, group, turn, step], x_sem.at[1, group, turn, step], "vec", vec_at(step)
                )
            )
        across[group, turn, 0] = begin(
            remote(at, at, p_sem.at[0, group, turn], p_sem.at[1, group, turn], "vec", partner)
        )

    forwards = []

    def forward(group, turn):
        for step in range(1, others):
            across[group, turn, step].wait_recv()
            at = gathered.at[vec_at(others - step), tile_at(tiles - turn), group]
            forwards.append(
                begin(
                    remote(
                        at, at, f_sem.at[0, group, turn, step], f_sem.at[1, group, turn, step], "vec", partner
                    )
                )
            )

    def steps_of(group):
        todo = [lambda: share(group, 0)]
        for turn in range(1, tiles):
            todo.append(lambda turn=turn: (share(group, turn), forward(group, turn - 1)))
        todo.append(lambda: forward(group, tiles - 1))
        return todo

    todo = []
    for group in range(groups):
        own_field[group].wait()
        for copy in sent[group]:
            copy.wait_recv()
        buffers = [field.at[group], first.at[group], second]
        hop(buffers[0], None, buffers[1])
        for order in range(1, ITERS):
            if order >= 2 and len(todo) > 0:
                todo.pop(0)()
            hop(buffers[1], buffers[0], buffers[2])
            buffers = [buffers[1], buffers[2], buffers[0]]
        done = buffers[1]
        returned[group, 0] = pltpu.make_async_copy(
            done.at[slab(me)], gathered.at[vec, me, group], local_sem.at[1 + groups + group]
        )
        returned[group, 0].start()
        for turn in range(1, tiles):
            returned[group, turn] = begin(
                remote(
                    done.at[slab(tile_at(turn))],
                    gathered.at[vec, me, group],
                    back_sem.at[0, group, turn],
                    back_sem.at[1, group, turn],
                    "tile",
                    tile_at(turn),
                )
            )
        todo += steps_of(group)
        todo.pop(0)()
    for step in todo:
        step()
    for group in range(groups):
        for turn in range(tiles):
            across[group, turn, 0].wait_recv()
    for copy in forwards:
        copy.wait_recv()
    for copy in waits:
        copy.wait_send()


def split(value):
    high = value.astype(jnp.bfloat16)
    low = (value - high.astype(jnp.float32)).astype(jnp.bfloat16)
    return high, low


def displace_kernel(dirs_ref, gathered, before, after, links_ref, back_ref, out_ref, cols_ref, sems):
    chunks, disps = out_ref.shape[0], out_ref.shape[1]
    tiles, groups, size = cols_ref.shape[0], cols_ref.shape[1], cols_ref.shape[4]
    pieces = tiles * groups
    vec = lax.axis_index("vec")
    copies = [
        pltpu.make_async_copy(before, cols_ref.at[:, :, 0:PER_PLANE], sems.at[0]),
        pltpu.make_async_copy(
            gathered.at[vec], cols_ref.at[:, :, PER_PLANE : PER_PLANE + chunks], sems.at[1]
        ),
        pltpu.make_async_copy(
            after, cols_ref.at[:, :, PER_PLANE + chunks : 2 * PER_PLANE + chunks], sems.at[2]
        ),
    ]
    for copy in copies:
        copy.start()
    for copy in copies:
        copy.wait()
    unrolled = math.gcd(pieces, 4)
    for disp in range(disps):
        for heading in range(6):
            @pl.when(dirs_ref[disp] == heading)
            def _(disp=disp, heading=heading):
                spatial = heading % 3
                step = 1 if heading < 3 else -1
                table = links_ref if step > 0 else back_ref

                @pl.loop(0, chunks * (pieces // unrolled))
                def _(index):
                    chunk = index % chunks
                    results = []
                    for inner in range(unrolled):
                        piece = index // chunks * unrolled + inner
                        part = lambda where, comp: cols_ref[
                            piece // groups, piece % groups, where + PER_PLANE, comp
                        ]
                        source = moved(part, chunk, spatial, step, chunk + step * PER_PLANE)
                        total = apply_link(table, chunk, spatial, step < 0, source, [None] * 6)
                        results.append((piece, total))
                    for piece, total in results:
                        home = pl.multiple_of(piece * size, size)
                        for comp in range(6):
                            out_ref[chunk, disp, comp, pl.ds(home, size), :] = total[comp]


def contract_kernel(tiles, gathered, shifted, cos_ref, sin_ref, out_ref, *scratch):
    staged, rows, left_hi, left_lo, right_hi, right_lo, part, got, load_sem, sum_sem = scratch
    chunks, disps, columns = shifted.shape[0], shifted.shape[1], shifted.shape[3]
    vecs, tile_count, groups, size = staged.shape[1], staged.shape[2], staged.shape[3], staged.shape[5]
    row_count = left_hi.shape[1]
    share = row_count // tiles
    width = right_hi.shape[1]
    some = width // (disps * columns)
    blocks = part.shape[0]
    me = lax.axis_index("tile")
    tile_at = lambda turn: (me + turn) % tiles

    def load(chunk):
        return pltpu.make_async_copy(
            gathered.at[:, :, :, chunk], staged.at[chunk % 2], load_sem.at[chunk % 2]
        )

    load(0).start()
    greet([("tile", tile_at(turn)) for turn in range(1, tiles)])

    @pl.loop(0, chunks)
    def _(chunk):
        @pl.when(chunk + 1 < chunks)
        def _():
            load(chunk + 1).start()

        load(chunk).wait()
        slot = chunk % 2
        if size % 8 == 0:
            flat = lambda comp: staged[slot, :, :, :, comp].reshape(row_count, LANES)
        else:
            for vec in range(vecs):
                for tile in range(tile_count):
                    for group in range(groups):
                        place = ((vec * tile_count + tile) * groups + group) * size
                        for comp in range(6):
                            rows[comp, place : place + size, :] = staged[
                                slot, vec, tile, group, comp
                            ]
            flat = lambda comp: rows[comp]
        for colour in range(3):
            at = pl.ds(pl.multiple_of((chunk * 3 + colour) * LANES, LANES), LANES)
            real, imag = flat(colour), flat(3 + colour)
            for kind, value in enumerate((real, imag, real + imag)):
                left_hi[kind, :, at], left_lo[kind, :, at] = split(value)

    dims = (((1,), (1,)), ((), ()))
    dot = functools.partial(
        lax.dot_general, dimension_numbers=dims, preferred_element_type=jnp.float32
    )

    def parcel(block, turn):
        return remote(
            part.at[block, tile_at(turn)],
            got.at[block, me],
            sum_sem.at[0, block, turn],
            sum_sem.at[1, block, turn],
            "tile",
            tile_at(turn),
        )

    @pl.loop(0, blocks)
    def _(block):
        @pl.loop(0, chunks)
        def _(chunk):
            for p in range(some):
                c = cos_ref[chunk, pl.ds(block * some + p, 1), :]
                s = sin_ref[chunk, pl.ds(block * some + p, 1), :]
                for disp in range(disps):
                    place = (p * disps + disp) * columns
                    home = slice(place, place + columns)
                    for colour in range(3):
                        at = pl.ds(pl.multiple_of((chunk * 3 + colour) * LANES, LANES), LANES)
                        dr = shifted[chunk, disp, colour]
                        di = shifted[chunk, disp, 3 + colour]
                        real = c * dr + s * di
                        imag = c * di - s * dr
                        for kind, value in enumerate((real, imag, imag - real)):
                            high, low = split(value)
                            right_hi[kind, home, at] = high
                            right_lo[kind, home, at] = low

        def product(kind):
            return (
                dot(left_hi[kind], right_lo[kind])
                + dot(left_lo[kind], right_hi[kind])
                + dot(left_hi[kind], right_hi[kind])
            )

        first = product(0)
        second = product(1)
        both = product(2) + first - second
        total = first + second
        for tile in range(tiles):
            part[block, tile, 0] = total[tile * share : (tile + 1) * share]
            part[block, tile, 1] = both[tile * share : (tile + 1) * share]
        for turn in range(1, tiles):
            parcel(block, turn).start()

    for block in range(blocks):
        sums = [part[block, me, kind] for kind in range(2)]
        for turn in range(1, tiles):
            parcel(block, turn).wait_recv()
        for turn in range(1, tiles):
            for kind in range(2):
                sums[kind] = sums[kind] + got[block, tile_at(turn), kind]
        for kind in range(2):
            out_ref[kind, :, block * width : (block + 1) * width] = sums[kind]
    for block in range(blocks):
        for turn in range(1, tiles):
            parcel(block, turn).wait_send()


def phases(momenta, flat_index, extent_x):
    coord_x = flat_index // PLANE
    coord_y = flat_index % PLANE // LZ
    coord_z = flat_index % LZ
    part_x = jnp.mod(momenta[:, 0:1] * coord_x[None], extent_x).astype(jnp.float32) / extent_x
    part_y = jnp.mod(momenta[:, 1:2] * coord_y[None], LY).astype(jnp.float32) / LY
    part_z = jnp.mod(momenta[:, 2:3] * coord_z[None], LZ).astype(jnp.float32) / LZ
    angle = 2.0 * math.pi * (part_x + part_y + part_z)
    return (jnp.cos(angle), jnp.sin(angle))


def local(vectors, links, momenta, directions):
    nv = vectors.shape[1]
    sites = vectors.shape[3]
    tiles = lax.axis_size("tile")
    vecs = lax.axis_size("vec")
    disps = directions.shape[0]
    moms = momenta.shape[0]
    chunks = sites // LANES
    every = chunks * tiles
    share = nv // tiles
    norm = 1.0 / math.sqrt(3.0 * sites * tiles)
    me = lax.axis_index("tile")
    groups = 2 if share % 16 == 0 else 1
    size = share // groups
    some_chunks = chunks // vecs

    own_links = links.reshape(3, 18, chunks, LANES).transpose(2, 0, 1, 3)
    quarter = lax.dynamic_slice_in_dim(
        own_links, lax.axis_index("vec") * some_chunks, some_chunks, 0
    )
    field = vectors.reshape(2, tiles, groups, size, 3, chunks, LANES)
    field = field.transpose(2, 1, 5, 0, 4, 3, 6)
    field = field.reshape(groups, tiles, chunks, 6, size, LANES)

    vmem = pl.BlockSpec(memory_space=pltpu.VMEM)
    smem = pl.BlockSpec(memory_space=pltpu.SMEM)
    anywhere = pl.BlockSpec(memory_space=pl.ANY)
    f32 = lambda *shape: jax.ShapeDtypeStruct(shape, jnp.float32)
    room = lambda *shape: pltpu.VMEM(shape, jnp.float32)
    half = lambda *shape: pltpu.VMEM(shape, jnp.bfloat16)
    dma = lambda *shape: pltpu.SemaphoreType.DMA(shape)
    others = vecs // CORES
    gathered, own_back = pl.pallas_call(
        functools.partial(spread_kernel, tiles, vecs),
        out_shape=(
            f32(vecs, tiles, groups, chunks, 6, size, LANES),
            f32(chunks, 3, 18, LANES),
        ),
        in_specs=[anywhere, anywhere],
        out_specs=(anywhere, vmem),
        scratch_shapes=[
            room(groups, every, 6, size, LANES),
            room(groups, every, 6, size, LANES),
            room(every, 6, size, LANES),
            room(tiles, vecs, some_chunks, 3, 18, LANES),
            room(every, 3, 18, LANES),
            room(every, 3, 18, LANES),
            dma(1 + 2 * groups),
            dma(2, tiles),
            dma(2, max(others, 1)),
            dma(2),
            dma(2, max(others, 1)),
            dma(2, groups, tiles),
            dma(2, groups, tiles),
            dma(2, groups, tiles, max(others, 1)),
            dma(2, groups, tiles),
            dma(2, groups, tiles, max(others, 1)),
        ],
        compiler_params=pltpu.CompilerParams(
            vmem_limit_bytes=VMEM_LIMIT, collective_id=0, has_side_effects=True
        ),
        name="spread",
    )(quarter, field)

    def passed(value, steps):
        return lax.ppermute(value, "tile", [(i, (i + steps) % tiles) for i in range(tiles)])

    def halo(heading, steps, first):
        def fetch(value):
            own = lax.dynamic_index_in_dim(value, lax.axis_index("vec"), 0, False)
            return passed(own[:, :, first : first + PER_PLANE], steps)

        def nothing(value):
            return jnp.zeros((tiles, groups, PER_PLANE, 6, size, LANES), jnp.float32)

        return lax.cond(jnp.any(directions == heading), fetch, nothing, gathered)

    before = halo(3, 1, chunks - PER_PLANE)
    after = halo(0, -1, 0)

    flat_index = me * sites + jnp.arange(sites, dtype=jnp.int32)
    cosine, sine = phases(momenta, flat_index, sites * tiles // PLANE)
    cosine = (cosine * norm).reshape(moms, chunks, LANES).transpose(1, 0, 2)
    sine = (sine * norm).reshape(moms, chunks, LANES).transpose(1, 0, 2)

    displaced = pl.pallas_call(
        displace_kernel,
        out_shape=f32(chunks, disps, 6, nv, LANES),
        in_specs=[smem, anywhere, anywhere, anywhere, vmem, vmem],
        out_specs=vmem,
        scratch_shapes=[
            room(tiles, groups, chunks + 2 * PER_PLANE, 6, size, LANES),
            dma(3),
        ],
        compiler_params=pltpu.CompilerParams(vmem_limit_bytes=VMEM_LIMIT),
        name="displace",
    )(directions, gathered, before, after, own_links, own_back)

    row_count = nv * vecs
    some = max(1, min(moms, 256 // (disps * nv)))
    blocks = moms // some
    width = some * disps * nv
    depth = 3 * sites
    mine = pl.pallas_call(
        functools.partial(contract_kernel, tiles),
        out_shape=f32(2, row_count // tiles, moms * disps * nv),
        in_specs=[anywhere, vmem, vmem, vmem],
        out_specs=vmem,
        scratch_shapes=[
            room(2, vecs, tiles, groups, 6, size, LANES),
            room(6, row_count, LANES) if size % 8 else room(1, 8, LANES),
            half(3, row_count, depth),
            half(3, row_count, depth),
            half(3, width, depth),
            half(3, width, depth),
            room(blocks, tiles, 2, row_count // tiles, width),
            room(blocks, tiles, 2, row_count // tiles, width),
            dma(2),
            dma(2, blocks, tiles),
        ],
        compiler_params=pltpu.CompilerParams(
            vmem_limit_bytes=VMEM_LIMIT, collective_id=1, has_side_effects=True
        ),
        name="contract",
    )(gathered, displaced, cosine, sine)
    mine = mine.reshape(2, row_count // tiles, moms, disps, nv)
    return mine.transpose(1, 3, 0, 2, 4)


def solution(mesh):
    return jax.shard_map(
        local,
        mesh=mesh,
        in_specs=(
            P(None, "vec", None, ("groups", "tile")),
            P(None, None, None, None, ("groups", "tile")),
            P(),
            P(),
        ),
        out_specs=P(("groups", "tile"), None, None, None, "vec"),
        check_vma=False,
    )
```

```python
import functools
import math

import jax
import jax.numpy as jnp
from jax import lax
from jax.experimental import pallas as pl
from jax.experimental.pallas import tpu as pltpu
from jax.sharding import PartitionSpec as P

LY = 16
LZ = 32
ITERS = 4
PLANE = LY * LZ
LANES = 128
PER_PLANE = PLANE // LANES
HOP_SCALE = 0.125
VMEM_LIMIT = 60 * 1024 * 1024
CORES = 2
MESH = pl.DeviceIdType.MESH


def lane_index(like):
    return lax.broadcasted_iota(jnp.int32, like.shape, len(like.shape) - 1)


def shift_z(value, step):
    axis = len(value.shape) - 1
    lane = lane_index(value) % LZ
    if step > 0:
        plain = pltpu.roll(value, LANES - 1, axis)
        wrapped = pltpu.roll(value, LZ - 1, axis)
        return jnp.where(lane == LZ - 1, wrapped, plain)
    plain = pltpu.roll(value, 1, axis)
    wrapped = pltpu.roll(value, LANES - LZ + 1, axis)
    return jnp.where(lane == 0, wrapped, plain)


def shift_y(value, other, step):
    axis = len(value.shape) - 1
    lane = lane_index(value)
    if step > 0:
        return pltpu.roll(jnp.where(lane < LZ, other, value), LANES - LZ, axis)
    return pltpu.roll(jnp.where(lane >= LANES - LZ, other, value), LZ, axis)


def in_plane(chunk, step):
    base = chunk // PER_PLANE * PER_PLANE
    return base + (chunk + step + PER_PLANE) % PER_PLANE


def link_row(links, chunk, spatial, part, row, column):
    index = (part * 3 + row) * 3 + column
    return links[chunk, spatial, index : index + 1, :]


def apply_link(links, chunk, spatial, dagger, field, total):
    for row in range(3):
        real, imag = total[row], total[3 + row]
        for column in range(3):
            a, b = (column, row) if dagger else (row, column)
            lr = link_row(links, chunk, spatial, 0, a, b)
            li = link_row(links, chunk, spatial, 1, a, b)
            vr, vi = field[column], field[3 + column]
            if dagger:
                dr = lr * vr + li * vi
                di = lr * vi - li * vr
            else:
                dr = lr * vr - li * vi
                di = lr * vi + li * vr
            real = dr if real is None else real + dr
            imag = di if imag is None else imag + di
        total[row], total[3 + row] = real, imag
    return total


def moved(read, chunk, spatial, step, ahead_x):
    if spatial == 0:
        return [read(ahead_x, comp) for comp in range(6)]
    if spatial == 1:
        other = in_plane(chunk, step)
        return [shift_y(read(chunk, comp), read(other, comp), step) for comp in range(6)]
    return [shift_z(read(chunk, comp), step) for comp in range(6)]


def remote(src, dst, send, recv, axis, device):
    return pltpu.make_async_remote_copy(
        src_ref=src,
        dst_ref=dst,
        send_sem=send,
        recv_sem=recv,
        device_id={axis: device},
        device_id_type=MESH,
    )


def greet(places):
    barrier = pltpu.get_barrier_semaphore()
    for axis, device in places:
        pl.semaphore_signal(barrier, inc=1, device_id={axis: device}, device_id_type=MESH)
    pl.semaphore_wait(barrier, len(places))


def spread_kernel(tiles, vecs, links_in, field_in, gathered, own_table, *scratch):
    field, first, second, pieces, links, back, *sems = scratch
    local_sem, link_z, link_x, link_p, link_f, out_sem, back_sem, x_sem, p_sem, f_sem = sems
    groups, every = field.shape[0], field.shape[1]
    chunks = every // tiles
    some = pieces.shape[2]
    me, vec = lax.axis_index("tile"), lax.axis_index("vec")
    partner = vec + 1 - 2 * (vec % CORES)
    others = vecs // CORES
    tile_at = lambda turn: (me + turn) % tiles
    vec_at = lambda turn: (vec + CORES * turn) % vecs
    slab = lambda tile: pl.ds(tile * chunks, chunks)

    greet(
        [("tile", tile_at(turn)) for turn in range(1, tiles)]
        + [("vec", vec_at(turn)) for turn in range(1, others)]
        + [("vec", partner)]
    )

    waits = []

    def begin(copy):
        copy.start()
        waits.append(copy)
        return copy

    own_links = pltpu.make_async_copy(links_in, pieces.at[me, vec], local_sem.at[0])
    own_links.start()
    links_z = [
        begin(remote(links_in, pieces.at[me, vec], link_z.at[0, turn], link_z.at[1, turn], "tile", tile_at(turn)))
        for turn in range(1, tiles)
    ]
    own_field, sent = [], []
    for group in range(groups):
        own_field.append(
            pltpu.make_async_copy(
                field_in.at[group, me], field.at[group, slab(me)], local_sem.at[1 + group]
            )
        )
        own_field[group].start()
        sent.append(
            [
                begin(
                    remote(
                        field_in.at[group, tile_at(turn)],
                        field.at[group, slab(me)],
                        out_sem.at[0, group, turn],
                        out_sem.at[1, group, turn],
                        "tile",
                        tile_at(turn),
                    )
                )
                for turn in range(1, tiles)
            ]
        )

    own_links.wait()
    for copy in links_z:
        copy.wait_recv()
    mine = pieces.at[:, vec]
    links_x = [
        begin(remote(mine, mine, link_x.at[0, turn], link_x.at[1, turn], "vec", vec_at(turn)))
        for turn in range(1, others)
    ]
    links_p = begin(remote(mine, mine, link_p.at[0], link_p.at[1], "vec", partner))
    links_f = []
    for turn in range(1, others):
        links_x[turn - 1].wait_recv()
        got = pieces.at[:, vec_at(others - turn)]
        links_f.append(
            begin(remote(got, got, link_f.at[0, turn], link_f.at[1, turn], "vec", partner))
        )
    links_p.wait_recv()
    for copy in links_f:
        copy.wait_recv()

    @pl.loop(0, every)
    def _(chunk):
        place = chunk % chunks
        links[chunk] = pieces[chunk // chunks, place // some, place % some]

    @pl.loop(0, every)
    def _(chunk):
        back[chunk, 0] = links[(chunk - PER_PLANE + every) % every, 0]
        back[chunk, 1] = shift_y(links[chunk, 1], links[in_plane(chunk, -1), 1], -1)
        back[chunk, 2] = shift_z(links[chunk, 2], -1)

    @pl.loop(0, chunks)
    def _(chunk):
        for spatial in range(3):
            at = me * chunks + chunk
            own_table[spatial, chunk] = links[at, spatial]
            for part in range(2):
                for row in range(3):
                    for column in range(3):
                        place = (part * 3 + row) * 3 + column
                        value = link_row(back, at, spatial, part, column, row)
                        own_table[3 + spatial, chunk, place : place + 1, :] = -value if part else value

    def hop(source, previous, target):
        @pl.loop(0, every)
        def _(chunk):
            read = lambda at, comp: source[at, comp]
            total = [None] * 6
            for spatial in range(3):
                ahead = moved(read, chunk, spatial, 1, (chunk + PER_PLANE) % every)
                total = apply_link(links, chunk, spatial, False, ahead, total)
                behind = moved(
                    read, chunk, spatial, -1, (chunk - PER_PLANE + every) % every
                )
                total = apply_link(back, chunk, spatial, True, behind, total)
            for comp in range(6):
                if previous is None:
                    target[chunk, comp] = HOP_SCALE * total[comp]
                else:
                    target[chunk, comp] = (
                        2.0 * HOP_SCALE * total[comp] - previous[chunk, comp]
                    )

    returned, across = {}, {}

    def share(group, turn):
        if turn > 0:
            returned[group, turn].wait_recv()
        else:
            returned[group, turn].wait()
        at = gathered.at[vec, tile_at(tiles - turn), group]
        for step in range(1, others):
            across[group, turn, step] = begin(
                remote(
                    at, at, x_sem.at[0, group, turn, step], x_sem.at[1, group, turn, step], "vec", vec_at(step)
                )
            )
        across[group, turn, 0] = begin(
            remote(at, at, p_sem.at[0, group, turn], p_sem.at[1, group, turn], "vec", partner)
        )

    forwards = []

    def forward(group, turn):
        for step in range(1, others):
            across[group, turn, step].wait_recv()
            at = gathered.at[vec_at(others - step), tile_at(tiles - turn), group]
            forwards.append(
                begin(
                    remote(
                        at, at, f_sem.at[0, group, turn, step], f_sem.at[1, group, turn, step], "vec", partner
                    )
                )
            )

    def steps_of(group):
        todo = [lambda: share(group, 0)]
        for turn in range(1, tiles):
            todo.append(lambda turn=turn: (share(group, turn), forward(group, turn - 1)))
        todo.append(lambda: forward(group, tiles - 1))
        return todo

    todo = []
    for group in range(groups):
        own_field[group].wait()
        for copy in sent[group]:
            copy.wait_recv()
        buffers = [field.at[group], first.at[group], second]
        hop(buffers[0], None, buffers[1])
        for order in range(1, ITERS):
            if order >= 2 and len(todo) > 0:
                todo.pop(0)()
            hop(buffers[1], buffers[0], buffers[2])
            buffers = [buffers[1], buffers[2], buffers[0]]
        done = buffers[1]
        returned[group, 0] = pltpu.make_async_copy(
            done.at[slab(me)], gathered.at[vec, me, group], local_sem.at[1 + groups + group]
        )
        returned[group, 0].start()
        for turn in range(1, tiles):
            returned[group, turn] = begin(
                remote(
                    done.at[slab(tile_at(turn))],
                    gathered.at[vec, me, group],
                    back_sem.at[0, group, turn],
                    back_sem.at[1, group, turn],
                    "tile",
                    tile_at(turn),
                )
            )
        todo += steps_of(group)
        todo.pop(0)()
    for step in todo:
        step()
    for group in range(groups):
        for turn in range(tiles):
            across[group, turn, 0].wait_recv()
    for copy in forwards:
        copy.wait_recv()
    for copy in waits:
        copy.wait_send()


def split(value):
    high = value.astype(jnp.bfloat16)
    low = (value - high.astype(jnp.float32)).astype(jnp.bfloat16)
    return high, low


def shifts(read, chunk):
    other = lambda step: in_plane(chunk, step)
    found = []
    for comp in range(6):
        here = read(chunk, comp)
        found.append(
            (
                read(chunk + PER_PLANE, comp),
                shift_y(here, read(other(1), comp), 1),
                shift_z(here, 1),
                read(chunk - PER_PLANE, comp),
                shift_y(here, read(other(-1), comp), -1),
                shift_z(here, -1),
            )
        )
    return found


def contract_kernel(
    tiles, dirs_ref, gathered, before, after, table, cos_ref, sin_ref, out_ref, *scratch
):
    cols, shifted, staged, rows, left_hi, left_lo, *scratch = scratch
    right_hi, right_lo, sums, part, got, load_sem, sum_sem = scratch[0:2], scratch[2:4], *scratch[4:]
    chunks, disps, columns = shifted.shape[0], shifted.shape[1], shifted.shape[3]
    vecs, tile_count, groups, size = staged.shape[1], staged.shape[2], staged.shape[3], staged.shape[5]
    row_count = left_hi.shape[1]
    share = row_count // tiles
    width, depth = right_hi[0].shape[1], right_hi[0].shape[2]
    span = depth // (3 * LANES)
    steps = chunks // span
    some = width // (disps * columns)
    blocks = part.shape[0]
    pieces = tile_count * groups
    me, vec = lax.axis_index("tile"), lax.axis_index("vec")

    def load(chunk):
        return pltpu.make_async_copy(
            gathered.at[:, :, :, chunk], staged.at[chunk % 2], load_sem.at[chunk % 2]
        )

    copies = [
        pltpu.make_async_copy(before, cols.at[:, :, 0:PER_PLANE], load_sem.at[2]),
        pltpu.make_async_copy(
            gathered.at[vec], cols.at[:, :, PER_PLANE : PER_PLANE + chunks], load_sem.at[3]
        ),
        pltpu.make_async_copy(
            after, cols.at[:, :, PER_PLANE + chunks : 2 * PER_PLANE + chunks], load_sem.at[4]
        ),
    ]
    for copy in copies:
        copy.start()
    load(0).start()
    up, down = jnp.minimum(me + 1, tiles - 1), jnp.maximum(me - 1, 0)
    greet([("tile", (me + turn) % tiles) for turn in range(1, tiles)])
    for copy in copies:
        copy.wait()

    unrolled = math.gcd(pieces, 4)

    @pl.loop(0, chunks * (pieces // unrolled))
    def _(index):
        chunk = index % chunks
        results = []
        for inner in range(unrolled):
            piece = index // chunks * unrolled + inner
            read = lambda where, comp, piece=piece: cols[
                piece // groups, piece % groups, where + PER_PLANE, comp
            ]
            found = shifts(read, chunk)
            home = pl.multiple_of(piece * size, size)
            for disp in range(disps):
                heading = dirs_ref[disp]
                source = []
                for comp in range(6):
                    value = found[comp][0]
                    for other in range(1, 6):
                        value = jnp.where(heading == other, found[comp][other], value)
                    source.append(value)
                for row in range(3):
                    real = imag = None
                    for column in range(3):
                        place = row * 3 + column
                        lr = table[heading, chunk, place : place + 1, :]
                        li = table[heading, chunk, 9 + place : 10 + place, :]
                        dr = lr * source[column] - li * source[3 + column]
                        di = lr * source[3 + column] + li * source[column]
                        real = dr if real is None else real + dr
                        imag = di if imag is None else imag + di
                    results.append((disp, row, home, real))
                    results.append((disp, 3 + row, home, imag))
        for disp, comp, home, value in results:
            shifted[chunk, disp, comp, pl.ds(home, size), :] = value

    @pl.loop(0, chunks)
    def _(chunk):
        @pl.when(chunk + 1 < chunks)
        def _():
            load(chunk + 1).start()

        load(chunk).wait()
        slot = chunk % 2
        if size % 8 == 0:
            flat = lambda comp: staged[slot, :, :, :, comp].reshape(row_count, LANES)
        else:
            for owner in range(vecs):
                for tile in range(tile_count):
                    for group in range(groups):
                        place = ((owner * tile_count + tile) * groups + group) * size
                        for comp in range(6):
                            rows[comp, place : place + size, :] = staged[
                                slot, owner, tile, group, comp
                            ]
            flat = lambda comp: rows[comp]
        for colour in range(3):
            at = pl.ds(pl.multiple_of((chunk * 3 + colour) * LANES, LANES), LANES)
            real, imag = flat(colour), flat(3 + colour)
            for kind, value in enumerate((real, imag, real + imag)):
                left_hi[kind, :, at], left_lo[kind, :, at] = split(value)

    dims = (((1,), (1,)), ((), ()))
    dot = functools.partial(
        lax.dot_general, dimension_numbers=dims, preferred_element_type=jnp.float32
    )

    def prepare(block, step, which):
        for inner in range(span):
            chunk = step * span + inner
            for p in range(some):
                c = cos_ref[chunk, pl.ds(block * some + p, 1), :]
                s = sin_ref[chunk, pl.ds(block * some + p, 1), :]
                for disp in range(disps):
                    place = (p * disps + disp) * columns
                    home = slice(place, place + columns)
                    for colour in range(3):
                        first = (inner * 3 + colour) * LANES
                        at = slice(first, first + LANES)
                        dr = shifted[chunk, disp, colour]
                        di = shifted[chunk, disp, 3 + colour]
                        real = c * dr + s * di
                        imag = c * di - s * dr
                        for kind, value in enumerate((real, imag, imag - real)):
                            high, low = split(value)
                            right_hi[which][kind, home, at] = high
                            right_lo[which][kind, home, at] = low

    def product(kind, step, which):
        at = slice(step * depth, (step + 1) * depth)
        high, low = left_hi[kind, :, at], left_lo[kind, :, at]
        right = right_hi[which][kind]
        return dot(high, right_lo[which][kind]) + dot(low, right) + dot(high, right)

    def parcel(block, target, device, way):
        return remote(
            part.at[block, target],
            got.at[way, block, target],
            sum_sem.at[way, 0, block, target],
            sum_sem.at[way, 1, block, target],
            "tile",
            device,
        )

    def serve(time):
        for way, (age, device) in enumerate(((me, up), (tiles - 1 - me, down))):
            block = time - age

            @pl.when((block >= 0) & (block < blocks))
            def _(way=way, age=age, device=device, block=block):
                for step in range(1, tiles):
                    target = tiles - step if way == 0 else step - 1

                    def receive(target=target):
                        parcel(block, target, device, way).wait_recv()
                        part[block, target] = part[block, target] + got[way, block, target]

                    ahead = me < target if way == 0 else me > target
                    pl.when(ahead & (age > 0))(receive)
                    pl.when(ahead)(lambda target=target: parcel(block, target, device, way).start())

    prepare(0, 0, 0)

    @pl.loop(0, blocks)
    def _(block):
        for step in range(steps):
            after_last = step + 1 == steps
            if steps % 2:
                prepare(block, step, step % 2)
            else:
                prepare(
                    jnp.minimum(block + 1, blocks - 1) if after_last else block,
                    0 if after_last else step + 1,
                    (step + 1) % 2,
                )
            for kind in range(3):
                value = product(kind, step, step % 2)
                sums[kind] = value if step == 0 else sums[kind] + value
        total = sums[0] + sums[1]
        both = sums[2] + sums[0] - sums[1]
        for tile in range(tiles):
            part[block, tile, 0] = total[tile * share : (tile + 1) * share]
            part[block, tile, 1] = both[tile * share : (tile + 1) * share]
        serve(block)

    @pl.loop(blocks, blocks + tiles - 1)
    def _(time):
        serve(time)

    for block in range(blocks):
        for way, (age, device) in enumerate(((me, up), (tiles - 1 - me, down))):

            @pl.when(age > 0)
            def _(way=way, device=device):
                parcel(block, me, device, way).wait_recv()
                part[block, me] = part[block, me] + got[way, block, me]

        for kind in range(2):
            out_ref[kind, :, block * width : (block + 1) * width] = part[block, me, kind]
        for target in range(tiles):
            pl.when(me < target)(lambda: parcel(block, target, up, 0).wait_send())
            pl.when(me > target)(lambda: parcel(block, target, down, 1).wait_send())


def phases(momenta, flat_index, extent_x):
    coord_x = flat_index // PLANE
    coord_y = flat_index % PLANE // LZ
    coord_z = flat_index % LZ
    part_x = jnp.mod(momenta[:, 0:1] * coord_x[None], extent_x).astype(jnp.float32) / extent_x
    part_y = jnp.mod(momenta[:, 1:2] * coord_y[None], LY).astype(jnp.float32) / LY
    part_z = jnp.mod(momenta[:, 2:3] * coord_z[None], LZ).astype(jnp.float32) / LZ
    angle = 2.0 * math.pi * (part_x + part_y + part_z)
    return (jnp.cos(angle), jnp.sin(angle))


def local(vectors, links, momenta, directions):
    nv = vectors.shape[1]
    sites = vectors.shape[3]
    tiles = lax.axis_size("tile")
    vecs = lax.axis_size("vec")
    disps = directions.shape[0]
    moms = momenta.shape[0]
    chunks = sites // LANES
    every = chunks * tiles
    share = nv // tiles
    norm = 1.0 / math.sqrt(3.0 * sites * tiles)
    me = lax.axis_index("tile")
    groups = 2 if share % 16 == 0 else 1
    size = share // groups
    some_chunks = chunks // vecs

    own_links = links.reshape(3, 18, chunks, LANES).transpose(2, 0, 1, 3)
    quarter = lax.dynamic_slice_in_dim(
        own_links, lax.axis_index("vec") * some_chunks, some_chunks, 0
    )
    field = vectors.reshape(2, tiles, groups, size, 3, chunks, LANES)
    field = field.transpose(2, 1, 5, 0, 4, 3, 6)
    field = field.reshape(groups, tiles, chunks, 6, size, LANES)

    vmem = pl.BlockSpec(memory_space=pltpu.VMEM)
    smem = pl.BlockSpec(memory_space=pltpu.SMEM)
    anywhere = pl.BlockSpec(memory_space=pl.ANY)
    f32 = lambda *shape: jax.ShapeDtypeStruct(shape, jnp.float32)
    room = lambda *shape: pltpu.VMEM(shape, jnp.float32)
    half = lambda *shape: pltpu.VMEM(shape, jnp.bfloat16)
    dma = lambda *shape: pltpu.SemaphoreType.DMA(shape)
    others = vecs // CORES
    gathered, table = pl.pallas_call(
        functools.partial(spread_kernel, tiles, vecs),
        out_shape=(
            f32(vecs, tiles, groups, chunks, 6, size, LANES),
            f32(6, chunks, 18, LANES),
        ),
        in_specs=[anywhere, anywhere],
        out_specs=(anywhere, vmem),
        scratch_shapes=[
            room(groups, every, 6, size, LANES),
            room(groups, every, 6, size, LANES),
            room(every, 6, size, LANES),
            room(tiles, vecs, some_chunks, 3, 18, LANES),
            room(every, 3, 18, LANES),
            room(every, 3, 18, LANES),
            dma(1 + 2 * groups),
            dma(2, tiles),
            dma(2, max(others, 1)),
            dma(2),
            dma(2, max(others, 1)),
            dma(2, groups, tiles),
            dma(2, groups, tiles),
            dma(2, groups, tiles, max(others, 1)),
            dma(2, groups, tiles),
            dma(2, groups, tiles, max(others, 1)),
        ],
        compiler_params=pltpu.CompilerParams(
            vmem_limit_bytes=VMEM_LIMIT, collective_id=0, has_side_effects=True
        ),
        name="spread",
    )(quarter, field)

    def passed(value, steps):
        return lax.ppermute(value, "tile", [(i, (i + steps) % tiles) for i in range(tiles)])

    def halo(heading, steps, first):
        def fetch(value):
            own = lax.dynamic_index_in_dim(value, lax.axis_index("vec"), 0, False)
            return passed(own[:, :, first : first + PER_PLANE], steps)

        def nothing(value):
            return jnp.zeros((tiles, groups, PER_PLANE, 6, size, LANES), jnp.float32)

        return lax.cond(jnp.any(directions == heading), fetch, nothing, gathered)

    before = halo(3, 1, chunks - PER_PLANE)
    after = halo(0, -1, 0)

    flat_index = me * sites + jnp.arange(sites, dtype=jnp.int32)
    cosine, sine = phases(momenta, flat_index, sites * tiles // PLANE)
    cosine = (cosine * norm).reshape(moms, chunks, LANES).transpose(1, 0, 2)
    sine = (sine * norm).reshape(moms, chunks, LANES).transpose(1, 0, 2)

    row_count = nv * vecs
    some = max(1, min(moms, 256 // (disps * nv)))
    blocks = moms // some
    width = some * disps * nv
    depth = 3 * sites
    span = 2 if chunks % 4 == 0 else chunks
    right = half(3, width, 3 * span * LANES)
    mine = pl.pallas_call(
        functools.partial(contract_kernel, tiles),
        out_shape=f32(2, row_count // tiles, moms * disps * nv),
        in_specs=[smem, anywhere, anywhere, anywhere, vmem, vmem, vmem],
        out_specs=vmem,
        scratch_shapes=[
            room(tiles, groups, chunks + 2 * PER_PLANE, 6, size, LANES),
            room(chunks, disps, 6, nv, LANES),
            room(2, vecs, tiles, groups, 6, size, LANES),
            room(6, row_count, LANES) if size % 8 else room(1, 8, LANES),
            half(3, row_count, depth),
            half(3, row_count, depth),
            right,
            right,
            right,
            right,
            room(3, row_count, width),
            room(blocks, tiles, 2, row_count // tiles, width),
            room(2, blocks, tiles, 2, row_count // tiles, width),
            dma(5),
            dma(2, 2, blocks, tiles),
        ],
        compiler_params=pltpu.CompilerParams(
            vmem_limit_bytes=VMEM_LIMIT, collective_id=1, has_side_effects=True
        ),
        name="contract",
    )(directions, gathered, before, after, table, cosine, sine)
    mine = mine.reshape(2, row_count // tiles, moms, disps, nv)
    return mine.transpose(1, 3, 0, 2, 4)


def solution(mesh):
    return jax.shard_map(
        local,
        mesh=mesh,
        in_specs=(
            P(None, "vec", None, ("groups", "tile")),
            P(None, None, None, None, ("groups", "tile")),
            P(),
            P(),
        ),
        out_specs=P(("groups", "tile"), None, None, None, "vec"),
        check_vma=False,
    )
```

```python
import functools
import math

import jax
import jax.numpy as jnp
from jax import lax
from jax.experimental import pallas as pl
from jax.experimental.pallas import tpu as pltpu
from jax.sharding import PartitionSpec as P

LY = 16
LZ = 32
ITERS = 4
PLANE = LY * LZ
LANES = 128
PER_PLANE = PLANE // LANES
HOP_SCALE = 0.125
VMEM_LIMIT = 60 * 1024 * 1024
CORES = 2
MESH = pl.DeviceIdType.MESH


def lane_index(like):
    return lax.broadcasted_iota(jnp.int32, like.shape, len(like.shape) - 1)


def shift_z(value, step):
    axis = len(value.shape) - 1
    lane = lane_index(value) % LZ
    if step > 0:
        plain = pltpu.roll(value, LANES - 1, axis)
        wrapped = pltpu.roll(value, LZ - 1, axis)
        return jnp.where(lane == LZ - 1, wrapped, plain)
    plain = pltpu.roll(value, 1, axis)
    wrapped = pltpu.roll(value, LANES - LZ + 1, axis)
    return jnp.where(lane == 0, wrapped, plain)


def shift_y(value, other, step):
    axis = len(value.shape) - 1
    lane = lane_index(value)
    if step > 0:
        return pltpu.roll(jnp.where(lane < LZ, other, value), LANES - LZ, axis)
    return pltpu.roll(jnp.where(lane >= LANES - LZ, other, value), LZ, axis)


def in_plane(chunk, step):
    base = chunk // PER_PLANE * PER_PLANE
    return base + (chunk + step + PER_PLANE) % PER_PLANE


def link_row(links, chunk, spatial, part, row, column):
    index = (part * 3 + row) * 3 + column
    return links[chunk, spatial, index : index + 1, :]


def apply_link(links, chunk, spatial, dagger, field, total):
    for row in range(3):
        real, imag = total[row], total[3 + row]
        for column in range(3):
            a, b = (column, row) if dagger else (row, column)
            lr = link_row(links, chunk, spatial, 0, a, b)
            li = link_row(links, chunk, spatial, 1, a, b)
            vr, vi = field[column], field[3 + column]
            if dagger:
                dr = lr * vr + li * vi
                di = lr * vi - li * vr
            else:
                dr = lr * vr - li * vi
                di = lr * vi + li * vr
            real = dr if real is None else real + dr
            imag = di if imag is None else imag + di
        total[row], total[3 + row] = real, imag
    return total


def moved(read, chunk, spatial, step, ahead_x):
    if spatial == 0:
        return [read(ahead_x, comp) for comp in range(6)]
    if spatial == 1:
        other = in_plane(chunk, step)
        return [shift_y(read(chunk, comp), read(other, comp), step) for comp in range(6)]
    return [shift_z(read(chunk, comp), step) for comp in range(6)]


def remote(src, dst, send, recv, axis, device):
    return pltpu.make_async_remote_copy(
        src_ref=src,
        dst_ref=dst,
        send_sem=send,
        recv_sem=recv,
        device_id={axis: device},
        device_id_type=MESH,
    )


def greet(places):
    barrier = pltpu.get_barrier_semaphore()
    for axis, device in places:
        pl.semaphore_signal(barrier, inc=1, device_id={axis: device}, device_id_type=MESH)
    pl.semaphore_wait(barrier, len(places))


def spread_kernel(tiles, vecs, links_in, field_in, gathered, own_table, *scratch):
    field, first, second, pieces, links, back, *sems = scratch
    local_sem, link_z, link_x, link_p, link_f, out_sem, back_sem, x_sem, p_sem, f_sem = sems
    groups, every = field.shape[0], field.shape[1]
    chunks = every // tiles
    some = pieces.shape[2]
    me, vec = lax.axis_index("tile"), lax.axis_index("vec")
    partner = vec + 1 - 2 * (vec % CORES)
    others = vecs // CORES
    tile_at = lambda turn: (me + turn) % tiles
    vec_at = lambda turn: (vec + CORES * turn) % vecs
    slab = lambda tile: pl.ds(tile * chunks, chunks)

    greet(
        [("tile", tile_at(turn)) for turn in range(1, tiles)]
        + [("vec", vec_at(turn)) for turn in range(1, others)]
        + [("vec", partner)]
    )

    waits = []

    def begin(copy):
        copy.start()
        waits.append(copy)
        return copy

    own_links = pltpu.make_async_copy(links_in, pieces.at[me, vec], local_sem.at[0])
    own_links.start()
    links_z = [
        begin(remote(links_in, pieces.at[me, vec], link_z.at[0, turn], link_z.at[1, turn], "tile", tile_at(turn)))
        for turn in range(1, tiles)
    ]
    own_field, sent = [], []
    for group in range(groups):
        own_field.append(
            pltpu.make_async_copy(
                field_in.at[group, me], field.at[group, slab(me)], local_sem.at[1 + group]
            )
        )
        own_field[group].start()
        sent.append(
            [
                begin(
                    remote(
                        field_in.at[group, tile_at(turn)],
                        field.at[group, slab(me)],
                        out_sem.at[0, group, turn],
                        out_sem.at[1, group, turn],
                        "tile",
                        tile_at(turn),
                    )
                )
                for turn in range(1, tiles)
            ]
        )

    own_links.wait()
    for copy in links_z:
        copy.wait_recv()
    mine = pieces.at[:, vec]
    links_x = [
        begin(remote(mine, mine, link_x.at[0, turn], link_x.at[1, turn], "vec", vec_at(turn)))
        for turn in range(1, others)
    ]
    links_p = begin(remote(mine, mine, link_p.at[0], link_p.at[1], "vec", partner))
    links_f = []
    for turn in range(1, others):
        links_x[turn - 1].wait_recv()
        got = pieces.at[:, vec_at(others - turn)]
        links_f.append(
            begin(remote(got, got, link_f.at[0, turn], link_f.at[1, turn], "vec", partner))
        )
    links_p.wait_recv()
    for copy in links_f:
        copy.wait_recv()

    @pl.loop(0, every)
    def _(chunk):
        place = chunk % chunks
        links[chunk] = pieces[chunk // chunks, place // some, place % some]

    @pl.loop(0, every)
    def _(chunk):
        back[chunk, 0] = links[(chunk - PER_PLANE + every) % every, 0]
        back[chunk, 1] = shift_y(links[chunk, 1], links[in_plane(chunk, -1), 1], -1)
        back[chunk, 2] = shift_z(links[chunk, 2], -1)

    @pl.loop(0, chunks)
    def _(chunk):
        for spatial in range(3):
            at = me * chunks + chunk
            own_table[spatial, chunk] = links[at, spatial]
            for part in range(2):
                for row in range(3):
                    for column in range(3):
                        place = (part * 3 + row) * 3 + column
                        value = link_row(back, at, spatial, part, column, row)
                        own_table[3 + spatial, chunk, place : place + 1, :] = -value if part else value

    pair = math.gcd(every, 2)

    def hop(source, previous, target):
        @pl.loop(0, every // pair)
        def _(index):
            read = lambda at, comp: source[at, comp]
            for inner in range(pair):
                chunk = index * pair + inner
                total = [None] * 6
                for spatial in range(3):
                    ahead = moved(read, chunk, spatial, 1, (chunk + PER_PLANE) % every)
                    total = apply_link(links, chunk, spatial, False, ahead, total)
                    behind = moved(
                        read, chunk, spatial, -1, (chunk - PER_PLANE + every) % every
                    )
                    total = apply_link(back, chunk, spatial, True, behind, total)
                for comp in range(6):
                    if previous is None:
                        target[chunk, comp] = HOP_SCALE * total[comp]
                    else:
                        target[chunk, comp] = (
                            2.0 * HOP_SCALE * total[comp] - previous[chunk, comp]
                        )

    returned, across = {}, {}

    def share(group, turn):
        if turn > 0:
            returned[group, turn].wait_recv()
        else:
            returned[group, turn].wait()
        at = gathered.at[vec, tile_at(tiles - turn), group]
        for step in range(1, others):
            across[group, turn, step] = begin(
                remote(
                    at, at, x_sem.at[0, group, turn, step], x_sem.at[1, group, turn, step], "vec", vec_at(step)
                )
            )
        across[group, turn, 0] = begin(
            remote(at, at, p_sem.at[0, group, turn], p_sem.at[1, group, turn], "vec", partner)
        )

    forwards = []

    def forward(group, turn):
        for step in range(1, others):
            across[group, turn, step].wait_recv()
            at = gathered.at[vec_at(others - step), tile_at(tiles - turn), group]
            forwards.append(
                begin(
                    remote(
                        at, at, f_sem.at[0, group, turn, step], f_sem.at[1, group, turn, step], "vec", partner
                    )
                )
            )

    def steps_of(group):
        todo = [lambda: share(group, 0)]
        for turn in range(1, tiles):
            todo.append(lambda turn=turn: (share(group, turn), forward(group, turn - 1)))
        todo.append(lambda: forward(group, tiles - 1))
        return todo

    todo = []
    for group in range(groups):
        own_field[group].wait()
        for copy in sent[group]:
            copy.wait_recv()
        buffers = [field.at[group], first.at[group], second]
        hop(buffers[0], None, buffers[1])
        for order in range(1, ITERS):
            if order >= 2 and len(todo) > 0:
                todo.pop(0)()
            hop(buffers[1], buffers[0], buffers[2])
            buffers = [buffers[1], buffers[2], buffers[0]]
        done = buffers[1]
        returned[group, 0] = pltpu.make_async_copy(
            done.at[slab(me)], gathered.at[vec, me, group], local_sem.at[1 + groups + group]
        )
        returned[group, 0].start()
        for turn in range(1, tiles):
            returned[group, turn] = begin(
                remote(
                    done.at[slab(tile_at(turn))],
                    gathered.at[vec, me, group],
                    back_sem.at[0, group, turn],
                    back_sem.at[1, group, turn],
                    "tile",
                    tile_at(turn),
                )
            )
        todo += steps_of(group)
        todo.pop(0)()
    for step in todo:
        step()
    for group in range(groups):
        for turn in range(tiles):
            across[group, turn, 0].wait_recv()
    for copy in forwards:
        copy.wait_recv()
    for copy in waits:
        copy.wait_send()


def split(value):
    high = value.astype(jnp.bfloat16)
    low = (value - high.astype(jnp.float32)).astype(jnp.bfloat16)
    return high, low


def shifts(read, chunk):
    other = lambda step: in_plane(chunk, step)
    found = []
    for comp in range(6):
        here = read(chunk, comp)
        found.append(
            (
                read(chunk + PER_PLANE, comp),
                shift_y(here, read(other(1), comp), 1),
                shift_z(here, 1),
                read(chunk - PER_PLANE, comp),
                shift_y(here, read(other(-1), comp), -1),
                shift_z(here, -1),
            )
        )
    return found


def contract_kernel(
    tiles, dirs_ref, gathered, before, after, table, cos_ref, sin_ref, out_ref, *scratch
):
    cols, shifted, staged, rows, left_hi, left_lo, *scratch = scratch
    right_hi, right_lo, sums, part, got, load_sem, sum_sem = scratch[0:2], scratch[2:4], *scratch[4:]
    chunks, disps, columns = shifted.shape[0], shifted.shape[1], shifted.shape[3]
    vecs, tile_count, groups, size = staged.shape[1], staged.shape[2], staged.shape[3], staged.shape[5]
    row_count = left_hi.shape[1]
    share = row_count // tiles
    width, depth = right_hi[0].shape[1], right_hi[0].shape[2]
    span = depth // (3 * LANES)
    steps = chunks // span
    some = width // (disps * columns)
    blocks = part.shape[0]
    pieces = tile_count * groups
    me, vec = lax.axis_index("tile"), lax.axis_index("vec")

    def load(chunk):
        return pltpu.make_async_copy(
            gathered.at[:, :, :, chunk], staged.at[chunk % 2], load_sem.at[chunk % 2]
        )

    copies = [
        pltpu.make_async_copy(before, cols.at[:, :, 0:PER_PLANE], load_sem.at[2]),
        pltpu.make_async_copy(
            gathered.at[vec], cols.at[:, :, PER_PLANE : PER_PLANE + chunks], load_sem.at[3]
        ),
        pltpu.make_async_copy(
            after, cols.at[:, :, PER_PLANE + chunks : 2 * PER_PLANE + chunks], load_sem.at[4]
        ),
    ]
    for copy in copies:
        copy.start()
    load(0).start()
    up, down = jnp.minimum(me + 1, tiles - 1), jnp.maximum(me - 1, 0)
    greet([("tile", (me + turn) % tiles) for turn in range(1, tiles)])
    for copy in copies:
        copy.wait()

    unrolled = math.gcd(pieces, 4)

    @pl.loop(0, chunks * (pieces // unrolled))
    def _(index):
        chunk = index % chunks
        results = []
        for inner in range(unrolled):
            piece = index // chunks * unrolled + inner
            read = lambda where, comp, piece=piece: cols[
                piece // groups, piece % groups, where + PER_PLANE, comp
            ]
            found = shifts(read, chunk)
            home = pl.multiple_of(piece * size, size)
            for disp in range(disps):
                heading = dirs_ref[disp]
                source = []
                for comp in range(6):
                    value = found[comp][0]
                    for other in range(1, 6):
                        value = jnp.where(heading == other, found[comp][other], value)
                    source.append(value)
                for row in range(3):
                    real = imag = None
                    for column in range(3):
                        place = row * 3 + column
                        lr = table[heading, chunk, place : place + 1, :]
                        li = table[heading, chunk, 9 + place : 10 + place, :]
                        dr = lr * source[column] - li * source[3 + column]
                        di = lr * source[3 + column] + li * source[column]
                        real = dr if real is None else real + dr
                        imag = di if imag is None else imag + di
                    results.append((disp, row, home, real))
                    results.append((disp, 3 + row, home, imag))
        for disp, comp, home, value in results:
            shifted[chunk, disp, comp, pl.ds(home, size), :] = value

    @pl.loop(0, chunks)
    def _(chunk):
        @pl.when(chunk + 1 < chunks)
        def _():
            load(chunk + 1).start()

        load(chunk).wait()
        slot = chunk % 2
        if size % 8 == 0:
            flat = lambda comp: staged[slot, :, :, :, comp].reshape(row_count, LANES)
        else:
            for owner in range(vecs):
                for tile in range(tile_count):
                    for group in range(groups):
                        place = ((owner * tile_count + tile) * groups + group) * size
                        for comp in range(6):
                            rows[comp, place : place + size, :] = staged[
                                slot, owner, tile, group, comp
                            ]
            flat = lambda comp: rows[comp]
        for colour in range(3):
            at = pl.ds(pl.multiple_of((chunk * 3 + colour) * LANES, LANES), LANES)
            real, imag = flat(colour), flat(3 + colour)
            for kind, value in enumerate((real, imag, real + imag)):
                left_hi[kind, :, at], left_lo[kind, :, at] = split(value)

    dims = (((1,), (1,)), ((), ()))
    dot = functools.partial(
        lax.dot_general, dimension_numbers=dims, preferred_element_type=jnp.float32
    )

    def prepare(block, step, which):
        for inner in range(span):
            chunk = step * span + inner
            for p in range(some):
                c = cos_ref[chunk, pl.ds(block * some + p, 1), :]
                s = sin_ref[chunk, pl.ds(block * some + p, 1), :]
                for disp in range(disps):
                    place = (p * disps + disp) * columns
                    home = slice(place, place + columns)
                    for colour in range(3):
                        first = (inner * 3 + colour) * LANES
                        at = slice(first, first + LANES)
                        dr = shifted[chunk, disp, colour]
                        di = shifted[chunk, disp, 3 + colour]
                        real = c * dr + s * di
                        imag = c * di - s * dr
                        for kind, value in enumerate((real, imag, imag - real)):
                            high, low = split(value)
                            right_hi[which][kind, home, at] = high
                            right_lo[which][kind, home, at] = low

    def product(kind, step, which):
        at = slice(step * depth, (step + 1) * depth)
        high, low = left_hi[kind, :, at], left_lo[kind, :, at]
        right = right_hi[which][kind]
        return dot(high, right_lo[which][kind]) + dot(low, right) + dot(high, right)

    def parcel(block, target, device, way):
        return remote(
            part.at[block, target],
            got.at[way, block, target],
            sum_sem.at[way, 0, block, target],
            sum_sem.at[way, 1, block, target],
            "tile",
            device,
        )

    def serve(time):
        for way, (age, device) in enumerate(((me, up), (tiles - 1 - me, down))):
            block = time - age

            @pl.when((block >= 0) & (block < blocks))
            def _(way=way, age=age, device=device, block=block):
                for step in range(1, tiles):
                    target = tiles - step if way == 0 else step - 1

                    def receive(target=target):
                        parcel(block, target, device, way).wait_recv()
                        part[block, target] = part[block, target] + got[way, block, target]

                    ahead = me < target if way == 0 else me > target
                    pl.when(ahead & (age > 0))(receive)
                    pl.when(ahead)(lambda target=target: parcel(block, target, device, way).start())

    prepare(0, 0, 0)

    @pl.loop(0, blocks)
    def _(block):
        for step in range(steps):
            after_last = step + 1 == steps
            if steps % 2:
                prepare(block, step, step % 2)
            else:
                prepare(
                    jnp.minimum(block + 1, blocks - 1) if after_last else block,
                    0 if after_last else step + 1,
                    (step + 1) % 2,
                )
            for kind in range(3):
                value = product(kind, step, step % 2)
                sums[kind] = value if step == 0 else sums[kind] + value
        total = sums[0] + sums[1]
        both = sums[2] + sums[0] - sums[1]
        for tile in range(tiles):
            part[block, tile, 0] = total[tile * share : (tile + 1) * share]
            part[block, tile, 1] = both[tile * share : (tile + 1) * share]
        serve(block)

    @pl.loop(blocks, blocks + tiles - 1)
    def _(time):
        serve(time)

    for block in range(blocks):
        for way, (age, device) in enumerate(((me, up), (tiles - 1 - me, down))):

            @pl.when(age > 0)
            def _(way=way, device=device):
                parcel(block, me, device, way).wait_recv()
                part[block, me] = part[block, me] + got[way, block, me]

        for kind in range(2):
            out_ref[kind, :, block * width : (block + 1) * width] = part[block, me, kind]
        for target in range(tiles):
            pl.when(me < target)(lambda: parcel(block, target, up, 0).wait_send())
            pl.when(me > target)(lambda: parcel(block, target, down, 1).wait_send())


def phases(momenta, flat_index, extent_x):
    coord_x = flat_index // PLANE
    coord_y = flat_index % PLANE // LZ
    coord_z = flat_index % LZ
    part_x = jnp.mod(momenta[:, 0:1] * coord_x[None], extent_x).astype(jnp.float32) / extent_x
    part_y = jnp.mod(momenta[:, 1:2] * coord_y[None], LY).astype(jnp.float32) / LY
    part_z = jnp.mod(momenta[:, 2:3] * coord_z[None], LZ).astype(jnp.float32) / LZ
    angle = 2.0 * math.pi * (part_x + part_y + part_z)
    return (jnp.cos(angle), jnp.sin(angle))


def local(vectors, links, momenta, directions):
    nv = vectors.shape[1]
    sites = vectors.shape[3]
    tiles = lax.axis_size("tile")
    vecs = lax.axis_size("vec")
    disps = directions.shape[0]
    moms = momenta.shape[0]
    chunks = sites // LANES
    every = chunks * tiles
    share = nv // tiles
    norm = 1.0 / math.sqrt(3.0 * sites * tiles)
    me = lax.axis_index("tile")
    groups = 2 if share % 16 == 0 else 1
    size = share // groups
    some_chunks = chunks // vecs

    own_links = links.reshape(3, 18, chunks, LANES).transpose(2, 0, 1, 3)
    quarter = lax.dynamic_slice_in_dim(
        own_links, lax.axis_index("vec") * some_chunks, some_chunks, 0
    )
    field = vectors.reshape(2, tiles, groups, size, 3, chunks, LANES)
    field = field.transpose(2, 1, 5, 0, 4, 3, 6)
    field = field.reshape(groups, tiles, chunks, 6, size, LANES)

    vmem = pl.BlockSpec(memory_space=pltpu.VMEM)
    smem = pl.BlockSpec(memory_space=pltpu.SMEM)
    anywhere = pl.BlockSpec(memory_space=pl.ANY)
    f32 = lambda *shape: jax.ShapeDtypeStruct(shape, jnp.float32)
    room = lambda *shape: pltpu.VMEM(shape, jnp.float32)
    half = lambda *shape: pltpu.VMEM(shape, jnp.bfloat16)
    dma = lambda *shape: pltpu.SemaphoreType.DMA(shape)
    others = vecs // CORES
    gathered, table = pl.pallas_call(
        functools.partial(spread_kernel, tiles, vecs),
        out_shape=(
            f32(vecs, tiles, groups, chunks, 6, size, LANES),
            f32(6, chunks, 18, LANES),
        ),
        in_specs=[anywhere, anywhere],
        out_specs=(anywhere, vmem),
        scratch_shapes=[
            room(groups, every, 6, size, LANES),
            room(groups, every, 6, size, LANES),
            room(every, 6, size, LANES),
            room(tiles, vecs, some_chunks, 3, 18, LANES),
            room(every, 3, 18, LANES),
            room(every, 3, 18, LANES),
            dma(1 + 2 * groups),
            dma(2, tiles),
            dma(2, max(others, 1)),
            dma(2),
            dma(2, max(others, 1)),
            dma(2, groups, tiles),
            dma(2, groups, tiles),
            dma(2, groups, tiles, max(others, 1)),
            dma(2, groups, tiles),
            dma(2, groups, tiles, max(others, 1)),
        ],
        compiler_params=pltpu.CompilerParams(
            vmem_limit_bytes=VMEM_LIMIT, collective_id=0, has_side_effects=True
        ),
        name="spread",
    )(quarter, field)

    def passed(value, steps):
        return lax.ppermute(value, "tile", [(i, (i + steps) % tiles) for i in range(tiles)])

    def halo(heading, steps, first):
        def fetch(value):
            own = lax.dynamic_index_in_dim(value, lax.axis_index("vec"), 0, False)
            return passed(own[:, :, first : first + PER_PLANE], steps)

        def nothing(value):
            return jnp.zeros((tiles, groups, PER_PLANE, 6, size, LANES), jnp.float32)

        return lax.cond(jnp.any(directions == heading), fetch, nothing, gathered)

    before = halo(3, 1, chunks - PER_PLANE)
    after = halo(0, -1, 0)

    flat_index = me * sites + jnp.arange(sites, dtype=jnp.int32)
    cosine, sine = phases(momenta, flat_index, sites * tiles // PLANE)
    cosine = (cosine * norm).reshape(moms, chunks, LANES).transpose(1, 0, 2)
    sine = (sine * norm).reshape(moms, chunks, LANES).transpose(1, 0, 2)

    row_count = nv * vecs
    some = max(1, min(moms, 256 // (disps * nv)))
    blocks = moms // some
    width = some * disps * nv
    depth = 3 * sites
    span = 2 if chunks % 4 == 0 else chunks
    right = half(3, width, 3 * span * LANES)
    mine = pl.pallas_call(
        functools.partial(contract_kernel, tiles),
        out_shape=f32(2, row_count // tiles, moms * disps * nv),
        in_specs=[smem, anywhere, anywhere, anywhere, vmem, vmem, vmem],
        out_specs=vmem,
        scratch_shapes=[
            room(tiles, groups, chunks + 2 * PER_PLANE, 6, size, LANES),
            room(chunks, disps, 6, nv, LANES),
            room(2, vecs, tiles, groups, 6, size, LANES),
            room(6, row_count, LANES) if size % 8 else room(1, 8, LANES),
            half(3, row_count, depth),
            half(3, row_count, depth),
            right,
            right,
            right,
            right,
            room(3, row_count, width),
            room(blocks, tiles, 2, row_count // tiles, width),
            room(2, blocks, tiles, 2, row_count // tiles, width),
            dma(5),
            dma(2, 2, blocks, tiles),
        ],
        compiler_params=pltpu.CompilerParams(
            vmem_limit_bytes=VMEM_LIMIT, collective_id=1, has_side_effects=True
        ),
        name="contract",
    )(directions, gathered, before, after, table, cosine, sine)
    mine = mine.reshape(2, row_count // tiles, moms, disps, nv)
    return mine.transpose(1, 3, 0, 2, 4)


def solution(mesh):
    return jax.shard_map(
        local,
        mesh=mesh,
        in_specs=(
            P(None, "vec", None, ("groups", "tile")),
            P(None, None, None, None, ("groups", "tile")),
            P(),
            P(),
        ),
        out_specs=P(("groups", "tile"), None, None, None, "vec"),
        check_vma=False,
    )
```
